32 devices in a mesh: dp: 4 (over y, x), gx: 2 (over core), gy: 4 (over z).
Axes of the slice: x: 2, y: 2, z: 4, core: 2. Of those that a mesh axis runs over, the one named last changes fastest.
Arguments:
- inputs: bfloat16 [8192, 1152], P(('dp', 'gy'), 'gx'), may hold values from -6 to 6
- segment_ids: int32 [8192], P('dp'), may hold values from 2047 to 8191, as said below
- positions: int32 [8192], P('dp'), may hold values from 0 to 2047, as said below
- attention_gain: float32 [1152], P('gx'), may hold values from 0.25 to 1.75
- qkv_weight: bfloat16 [1152, 1536], P('gx'), may hold values from -1 to 1
- query_gain: float32 [256], replicated, may hold values from 0.5 to 5
- key_gain: float32 [256], replicated, may hold values from 0.5 to 5
- out_weight: bfloat16 [1024, 1152], P(None, 'gx'), may hold values from -1.5 to 1.5
- feedforward_gain: float32 [1152], P('gx'), may hold values from 0.25 to 1.75
- gate_weight: bfloat16 [1152, 6912], P('gx', 'gy'), may hold values from -0.1875 to 0.1875
- up_weight: bfloat16 [1152, 6912], P('gx', 'gy'), may hold values from -0.1875 to 0.1875
- down_weight: bfloat16 [6912, 1152], P('gy', 'gx'), may hold values from -0.078125 to 0.078125
- grad_output: bfloat16 [8192, 1152], P(('dp', 'gy'), 'gx'), may hold values from -6 to 6
Outputs:
- output: bfloat16 [8192, 1152], P(('dp', 'gy'), 'gx')
- grad_inputs: float32 [8192, 1152], P(('dp', 'gy'), 'gx')
- grad_attention_gain: float32 [1152], P('gx')
- grad_qkv_weight: float32 [1152, 1536], P('gx', ('dp', 'gy'))
- grad_query_gain: float32 [256], replicated
- grad_key_gain: float32 [256], replicated
- grad_out_weight: float32 [1024, 1152], P(('dp', 'gy'), 'gx')
- grad_feedforward_gain: float32 [1152], P('gx')
- grad_gate_weight: float32 [1152, 6912], P('gx', 'gy')
- grad_up_weight: float32 [1152, 6912], P('gx', 'gy')
- grad_down_weight: float32 [6912, 1152], P('gy', 'gx')
The draws below stay inside these ranges and needn't reach their ends.
Inputs may be any that keep to these rules, and one draw needn't show every extreme that they name: `segment_ids`: each row of 2048 tokens is cut into segments of consecutive tokens, the last of them the row's tail; no segment id appears in two rows, ids never fall along a row, the tail of row r has id (r + 1) * 2048 - 1, and the first row is a single segment. `positions`: positions count 0, 1, 2 and so on from the first token of each segment.
All inputs are finite; a program needn't handle non-finite values.
Results may differ from the reference program's by a relative error of at most 0.03.
The reference program's roundings to bfloat16 on the way count: a program that leaves them out, or rounds other values in their place, can miss the bound.
Values may be sent and summed in bfloat16 or wider, within the bound.
A program may use at most 256 MiB of HBM per device.

```python
import jax
import jax.numpy as jnp
from jax import lax

D = 1152
HEADS = 4
HD = 256
FF = 6912
ROW_LEN = 2048
TOKENS = 8192
HQ = 1024
QKV = 1536


def packed_documents(key):
    base = jax.random.fold_in(key, 11)
    row_total = TOKENS // ROW_LEN
    breaks = jax.random.randint(jax.random.fold_in(base, 1), (row_total, ROW_LEN), 0, ROW_LEN // 4)
    tail_start = jax.random.randint(jax.random.fold_in(base, 2), (row_total, 1), ROW_LEN // 2, ROW_LEN)
    column = jnp.arange(ROW_LEN, dtype=jnp.int32)[None, :]
    row_number = jnp.arange(row_total, dtype=jnp.int32)[:, None]
    starts = (breaks == 0) | (column == 0) | (column == tail_start)
    starts = jnp.where(row_number == 0, column == 0, starts)
    start_count = starts.astype(jnp.int32)
    local_segment = jnp.cumsum(start_count, axis=1) - 1
    row_segments = jnp.sum(start_count, axis=1, keepdims=True)
    segment = row_number * ROW_LEN + ROW_LEN - row_segments + local_segment
    begin = lax.cummax(jnp.where(starts, column, 0), axis=1)
    position = column - begin
    return (segment.reshape(-1).astype(jnp.int32), position.reshape(-1).astype(jnp.int32))


def draw_segment_ids(key, part):
    return packed_documents(key)[0]


def draw_positions(key, part):
    return packed_documents(key)[1]


def draw_query_gain(key, part):
    sub_key = jax.random.fold_in(key, 21)
    return jax.random.uniform(sub_key, (HD,), jnp.float32, 0.5, 1.5)


def draw_key_gain(key, part):
    sub_key = jax.random.fold_in(key, 22)
    return jax.random.uniform(sub_key, (HD,), jnp.float32, 0.5, 1.5)


def draw_qkv_weight(key, part):
    base = jax.random.fold_in(key, 31)
    spread = D ** (-0.5)
    weights = jnp.clip(jax.random.normal(jax.random.fold_in(base, 1), (D, QKV), jnp.float32), -6.0, 6.0) * spread
    return weights.astype(jnp.bfloat16)


def steps_of(key, shape, split, low, largest):
    level = 1.0
    for dim, shards_of in split:
        draws = jax.random.uniform(jax.random.fold_in(jax.random.fold_in(key, 6), dim), (shards_of,), jnp.float32, low / len(split), largest / len(split))
        level = level * jnp.repeat(jnp.exp(draws), shape[dim] // shards_of).reshape((-1,) + (1,) * (len(shape) - 1 - dim))
    return level


def normal_values(key, shape, deviation, bound, cuts=(), kind=jnp.bfloat16):
    array = deviation * jax.random.normal(key, shape, jnp.float32)
    if cuts:
        array = array * steps_of(key, shape, cuts, -0.22, 0.18)
    return jnp.clip(array, -bound, bound).astype(kind)


def setup_inputs(seed: int = 0) -> dict:
    arg_keys = jax.random.split(jax.random.key(seed), 14)
    return {
        "inputs": normal_values(arg_keys[0], (TOKENS, D), 1.0, 6.0, ((0, 16), (1, 2))),
        "segment_ids": draw_segment_ids(jax.random.fold_in(arg_keys[13], 71), 0),
        "positions": draw_positions(jax.random.fold_in(arg_keys[13], 71), 0),
        "attention_gain": jnp.clip(1.0 + 0.15 * jax.random.normal(arg_keys[3], (D,), jnp.float32), 0.25, 1.75),
        "qkv_weight": draw_qkv_weight(jax.random.fold_in(arg_keys[13], 71), 0),
        "query_gain": draw_query_gain(jax.random.fold_in(arg_keys[13], 71), 0),
        "key_gain": draw_key_gain(jax.random.fold_in(arg_keys[13], 71), 0),
        "out_weight": normal_values(arg_keys[7], (HQ, D), (HD // 16) ** -0.5, 1.5, ((1, 2),)),
        "feedforward_gain": jnp.clip(1.0 + 0.15 * jax.random.normal(arg_keys[8], (D,), jnp.float32), 0.25, 1.75),
        "gate_weight": normal_values(arg_keys[9], (D, FF), D ** -0.5, 0.1875, ((0, 2), (1, 4))),
        "up_weight": normal_values(arg_keys[10], (D, FF), D ** -0.5, 0.1875, ((0, 2), (1, 4))),
        "down_weight": normal_values(arg_keys[11], (FF, D), FF ** -0.5, 0.078125, ((0, 4), (1, 2))),
        "grad_output": normal_values(arg_keys[12], (TOKENS, D), 1.0, 6.0, ((0, 16), (1, 2))),
    }


NORM_EPS = 1e-06
ROPE_BASE = 1000000.0
MASKED_SCORE = -1e+30

def rotate(tensor, token_pos):
    half_width = tensor.shape[-1] // 2
    frequency = ROPE_BASE ** (-(jnp.arange(half_width, dtype=jnp.float32) * 2.0 / tensor.shape[-1]))
    angles = token_pos.astype(jnp.float32)[:, None] * frequency[None, :]
    cosine = jnp.cos(angles)[:, None, :]
    sine_part = jnp.sin(angles)[:, None, :]
    first_half = tensor[..., :half_width]
    second_half = tensor[..., half_width:]
    return jnp.concatenate([first_half * cosine - second_half * sine_part, second_half * cosine + first_half * sine_part], axis=-1)

def prepare(projected, token_pos, gain_query, gain_key):
    row_count = projected.shape[0]
    queries = projected[:, :HEADS * HD].reshape(row_count, HEADS, HD)
    key_heads = projected[:, HEADS * HD:(HEADS + 1) * HD].reshape(row_count, 1, HD)
    values = projected[:, (HEADS + 1) * HD:]
    queries = queries * lax.rsqrt(lax.optimization_barrier(jnp.mean(queries * queries, axis=-1, keepdims=True)) + NORM_EPS) * gain_query
    key_heads = key_heads * lax.rsqrt(lax.optimization_barrier(jnp.mean(key_heads * key_heads, axis=-1, keepdims=True)) + NORM_EPS) * gain_key
    return (rotate(queries, token_pos), rotate(key_heads, token_pos)[:, 0, :], values)

def gelu_mix(gate_value, upper):
    return jax.nn.gelu(gate_value, approximate=True) * upper

def reference(inputs, segment_ids, positions, attention_gain, qkv_weight, query_gain, key_gain, out_weight, feedforward_gain, gate_weight, up_weight, down_weight, grad_output):
    f32 = jnp.float32
    bf16 = jnp.bfloat16
    scale = HD ** (-0.5)
    row_total = TOKENS // ROW_LEN

    def row_pass(state, row_data):
        inputs_row, seg_row, pos_row, grad_row = row_data
        inputs_f = inputs_row.astype(f32)
        attention_scale = lax.rsqrt(lax.optimization_barrier(jnp.mean(inputs_f * inputs_f, axis=-1, keepdims=True)) + NORM_EPS)
        normed_one = (inputs_f * attention_scale * attention_gain).astype(bf16)
        projected = jnp.dot(normed_one, qkv_weight, preferred_element_type=f32)

        def prep_local(proj_rows, gain_query, gain_key):
            return prepare(proj_rows, pos_row, gain_query, gain_key)
        (queries, key_rows_f, values), prep_back = jax.vjp(prep_local, projected, query_gain, key_gain)
        queries_b = queries.astype(bf16)
        keys_b = key_rows_f.astype(bf16)
        values_b = values.astype(bf16)
        allowed = (seg_row[:, None] == seg_row[None, :]) & (pos_row[None, :] <= pos_row[:, None])
        scores = jnp.einsum('qhd,kd->hqk', queries_b.astype(f32), keys_b.astype(f32)) * scale
        masked = jnp.where(allowed[None], scores, MASKED_SCORE)
        row_max = lax.optimization_barrier(jnp.max(masked, axis=-1, keepdims=True))
        log_total = row_max + jnp.log(lax.optimization_barrier(jnp.sum(jnp.where(allowed[None], jnp.exp(masked - row_max), 0.0), axis=-1, keepdims=True)))
        weights = jnp.where(allowed[None], jnp.exp(masked - log_total), 0.0)
        weights_b = weights.astype(bf16)
        attended = jnp.einsum('hqk,kd->qhd', weights_b.astype(f32), values_b.astype(f32))
        attended_b = attended.reshape(ROW_LEN, HQ).astype(bf16)
        hidden_one = inputs_f + jnp.dot(attended_b, out_weight, preferred_element_type=f32)
        feedforward_scale = lax.rsqrt(lax.optimization_barrier(jnp.mean(hidden_one * hidden_one, axis=-1, keepdims=True)) + NORM_EPS)
        normed_two = (hidden_one * feedforward_scale * feedforward_gain).astype(bf16)
        gate_value = jnp.dot(normed_two, gate_weight, preferred_element_type=f32)
        upper = jnp.dot(normed_two, up_weight, preferred_element_type=f32)
        activated_f, mix_back = jax.vjp(gelu_mix, gate_value, upper)
        activated = activated_f.astype(bf16)
        output_row = (hidden_one + jnp.dot(activated, down_weight, preferred_element_type=f32)).astype(bf16)
        grad_f = grad_row.astype(f32)
        grad_activated = jnp.dot(grad_row, down_weight.T, preferred_element_type=f32)
        grad_down = jnp.dot(activated.T, grad_row, preferred_element_type=f32)
        grad_gate_f, grad_upper_f = mix_back(grad_activated)
        grad_gate = grad_gate_f.astype(bf16)
        grad_upper = grad_upper_f.astype(bf16)
        grad_gate_w = jnp.dot(normed_two.T, grad_gate, preferred_element_type=f32)
        grad_up_w = jnp.dot(normed_two.T, grad_upper, preferred_element_type=f32)
        grad_normed_two = jnp.dot(grad_gate, gate_weight.T, preferred_element_type=f32) + jnp.dot(grad_upper, up_weight.T, preferred_element_type=f32)
        grad_ff_gain = lax.optimization_barrier(jnp.sum(grad_normed_two * hidden_one * feedforward_scale, axis=0))
        grad_hidden = grad_f + feedforward_scale * feedforward_gain * grad_normed_two - hidden_one * feedforward_scale ** 3 * lax.optimization_barrier(jnp.mean(grad_normed_two * feedforward_gain * hidden_one, axis=-1, keepdims=True))
        grad_hidden_b = grad_hidden.astype(bf16)
        grad_out_w = jnp.dot(attended_b.T, grad_hidden_b, preferred_element_type=f32)
        grad_attended = jnp.dot(grad_hidden_b, out_weight.T, preferred_element_type=f32).reshape(ROW_LEN, HEADS, HD)
        grad_attended_b = grad_attended.astype(bf16)
        correction = lax.optimization_barrier(jnp.sum(grad_attended * attended, axis=-1)).T
        grad_weights = jnp.einsum('qhd,kd->hqk', grad_attended_b.astype(f32), values_b.astype(f32))
        grad_scores = (weights * (grad_weights - correction[:, :, None])).astype(bf16)
        grad_queries = jnp.einsum('hqk,kd->qhd', grad_scores.astype(f32), keys_b.astype(f32)) * scale
        grad_keys = jnp.einsum('hqk,qhd->kd', grad_scores.astype(f32), queries_b.astype(f32)) * scale
        grad_values = jnp.einsum('hqk,qhd->kd', weights_b.astype(f32), grad_attended_b.astype(f32))
        grad_projected, grad_q_gain, grad_k_gain = prep_back((grad_queries, grad_keys, grad_values))
        grad_projected_b = grad_projected.astype(bf16)
        grad_qkv_w = jnp.dot(normed_one.T, grad_projected_b, preferred_element_type=f32)
        grad_normed_one = jnp.dot(grad_projected_b, qkv_weight.T, preferred_element_type=f32)
        grad_att_gain = lax.optimization_barrier(jnp.sum(grad_normed_one * inputs_f * attention_scale, axis=0))
        grad_inputs_row = grad_hidden + attention_scale * attention_gain * grad_normed_one - inputs_f * attention_scale ** 3 * lax.optimization_barrier(jnp.mean(grad_normed_one * attention_gain * inputs_f, axis=-1, keepdims=True))
        additions = (grad_att_gain, grad_qkv_w, grad_q_gain, grad_k_gain, grad_out_w, grad_ff_gain, grad_gate_w, grad_up_w, grad_down)
        state = tuple((held + added for held, added in zip(state, additions)))
        return (state, (output_row, grad_inputs_row))
    start_state = (jnp.zeros((D,), f32), jnp.zeros((D, QKV), f32), jnp.zeros((HD,), f32), jnp.zeros((HD,), f32), jnp.zeros((HQ, D), f32), jnp.zeros((D,), f32), jnp.zeros((D, FF), f32), jnp.zeros((D, FF), f32), jnp.zeros((FF, D), f32))
    rows_in = (inputs.reshape(row_total, ROW_LEN, D), segment_ids.reshape(row_total, ROW_LEN), positions.reshape(row_total, ROW_LEN), grad_output.reshape(row_total, ROW_LEN, D))
    sums, (output_rows, grad_rows) = lax.scan(row_pass, start_state, rows_in)
    return (output_rows.reshape(TOKENS, D), grad_rows.reshape(TOKENS, D), sums[0], sums[1], sums[2], sums[3], sums[4], sums[5], sums[6], sums[7], sums[8])
```

```python
import jax
import jax.numpy as jnp
from jax import lax
from jax.sharding import PartitionSpec as P

D = 1152
HEADS = 4
HD = 256
HQ = 1024


NORM_EPS = 1e-06
ROPE_BASE = 1000000.0
MASKED_SCORE = -1e30


def rotate(tensor, token_pos):
    half_width = tensor.shape[-1] // 2
    frequency = ROPE_BASE ** (-(jnp.arange(half_width, dtype=jnp.float32) * 2.0 / tensor.shape[-1]))
    angles = token_pos.astype(jnp.float32)[:, None] * frequency[None, :]
    cosine = jnp.cos(angles)[:, None, :]
    sine_part = jnp.sin(angles)[:, None, :]
    first_half = tensor[..., :half_width]
    second_half = tensor[..., half_width:]
    return jnp.concatenate(
        [
            first_half * cosine - second_half * sine_part,
            second_half * cosine + first_half * sine_part,
        ],
        axis=-1,
    )


def prepare(projected, token_pos, gain_query, gain_key):
    row_count = projected.shape[0]
    queries = projected[:, : HEADS * HD].reshape(row_count, HEADS, HD)
    key_heads = projected[:, HEADS * HD : (HEADS + 1) * HD].reshape(row_count, 1, HD)
    values = projected[:, (HEADS + 1) * HD :]
    queries = (
        queries
        * lax.rsqrt(jnp.mean(queries * queries, axis=-1, keepdims=True) + NORM_EPS)
        * gain_query
    )
    key_heads = (
        key_heads
        * lax.rsqrt(jnp.mean(key_heads * key_heads, axis=-1, keepdims=True) + NORM_EPS)
        * gain_key
    )
    return (rotate(queries, token_pos), rotate(key_heads, token_pos)[:, 0, :], values)


def gelu_mix(gate_value, upper):
    return jax.nn.gelu(gate_value, approximate=True) * upper


def partner(value):
    count = lax.axis_size("gx")
    return lax.ppermute(value, "gx", [(d, count - 1 - d) for d in range(count)])


def swap(value, axis_name, bit):
    count = lax.axis_size(axis_name)
    return lax.ppermute(value, axis_name, [(d, d ^ bit) for d in range(count)])


def pick(blocks, index, axis):
    return lax.dynamic_index_in_dim(blocks, index, axis, keepdims=False)


def both(value, axis):
    return jnp.concatenate([value, partner(value)], axis=axis)


def power_of_two(count):
    return count & (count - 1) == 0


def small_sum(value):
    for axis_name in ("dp", "gy"):
        count = lax.axis_size(axis_name)
        if not power_of_two(count):
            value = lax.psum(value, axis_name)
            continue
        bit = 1
        while bit < count:
            value = value + swap(value, axis_name, bit)
            bit *= 2
    return value


def scatter_pieces(blocks, order):
    index = lax.axis_index("dp")
    bits = (index // 2, index % 2)
    axes = [0, 1]
    for which in order:
        axis = axes.index(which)
        send = pick(blocks, 1 - bits[which], axis).astype(jnp.bfloat16)
        keep = pick(blocks, bits[which], axis).astype(jnp.float32)
        axes.remove(which)
        blocks = keep + swap(send, "dp", 2 - which).astype(jnp.float32)
    return blocks


def gather_pieces(block, order):
    index = lax.axis_index("dp")
    bits = (index // 2, index % 2)
    axes = []
    for which in reversed(order):
        other = swap(block, "dp", 2 - which)
        axes = sorted(axes + [which])
        axis = axes.index(which)
        block = jnp.where(
            bits[which] == 0,
            jnp.stack([block, other], axis=axis),
            jnp.stack([other, block], axis=axis),
        )
    return block


def rows_scatter_dp(total):
    rows, cols = total.shape
    count = lax.axis_size("dp")
    if count != 4:
        return lax.psum_scatter(total, "dp", scatter_dimension=0, tiled=True)
    blocks = total.reshape(2, 2, rows // 4, cols)
    half = rows // 8
    return jnp.concatenate(
        [
            scatter_pieces(blocks[:, :, :half], (0, 1)),
            scatter_pieces(blocks[:, :, half:], (1, 0)),
        ],
        axis=0,
    )


def sum_dp(total):
    rows, cols = total.shape
    count = lax.axis_size("dp")
    if count != 4 or rows % 8:
        return lax.psum(total.astype(jnp.bfloat16), "dp").astype(jnp.float32)
    halves = total.reshape(2, 2, 2, rows // 8, cols)
    pieces = [
        gather_pieces(scatter_pieces(halves[part], order).astype(jnp.bfloat16), order).reshape(
            rows // 2, cols
        )
        for part, order in ((0, (0, 1)), (1, (1, 0)))
    ]
    return jnp.concatenate(pieces, axis=0).astype(jnp.float32)


def gather_tokens(local_rows):
    return lax.all_gather(local_rows, "gy", axis=0, tiled=True)


def scatter_tokens(partial_rows):
    return lax.psum_scatter(
        partial_rows.astype(jnp.bfloat16), "gy", scatter_dimension=0, tiled=True
    ).astype(jnp.float32)


def norm_backward(residual_grad, grad_normed, inputs_f, inv_rms, gain):
    inner = jnp.sum(grad_normed * gain * inputs_f, axis=-1, keepdims=True)
    grad_in = residual_grad + inv_rms * gain * grad_normed - inputs_f * inv_rms**3 * inner / D
    return (grad_in, jnp.sum(grad_normed * inputs_f * inv_rms, axis=0))


def to_tokens(block):
    rows = block.shape[0] // 2
    mine = lax.axis_index("gx")
    halves = block.reshape(2, rows, block.shape[1])
    return jnp.concatenate([pick(halves, mine, 0), partner(pick(halves, 1 - mine, 0))], axis=1)


def to_widths(tokens):
    width = tokens.shape[1] // 2
    other = partner(tokens[:, width:])
    own = tokens[:, :width]
    return jnp.where(
        lax.axis_index("gx") == 0,
        jnp.concatenate([own, other], axis=0),
        jnp.concatenate([other, own], axis=0),
    )


def body(
    inputs,
    segment_ids,
    positions,
    attention_gain,
    qkv_weight,
    query_gain,
    key_gain,
    out_weight,
    feedforward_gain,
    gate_weight,
    up_weight,
    down_weight,
    grad_output,
):
    f32 = jnp.float32
    bf16 = jnp.bfloat16
    scale = HD ** (-0.5)
    dot = lambda a, b: jnp.dot(a, b, preferred_element_type=f32)
    groups_x = lax.axis_size("gx")
    groups_y = lax.axis_size("gy")
    assert groups_x == 2
    group_tokens = segment_ids.shape[0]
    per_device = group_tokens // (groups_x * groups_y)
    width = inputs.shape[1]
    index_x = lax.axis_index("gx")
    index_y = lax.axis_index("gy")

    def by_owner(token_values):
        grid = token_values.reshape(groups_y, groups_x, per_device)
        own = pick(grid, index_x, 1)
        keys = jnp.concatenate([own.reshape(-1), pick(grid, 1 - index_x, 1).reshape(-1)])
        return pick(own, index_y, 0), keys

    seg_query, seg_keys = by_owner(segment_ids)
    pos_query, pos_keys = by_owner(positions)
    allowed = (seg_query[:, None] == seg_keys[None, :]) & (pos_keys[None, :] <= pos_query[:, None])

    inputs_f = to_tokens(inputs).astype(f32)
    gains = both(jnp.stack([attention_gain, feedforward_gain]), 1)
    attention_gain_all, feedforward_gain_all = gains[0], gains[1]
    qkv_all = both(qkv_weight, 0)
    grad_out_own = to_tokens(grad_output)
    attention_scale = lax.rsqrt(
        jnp.sum(inputs_f * inputs_f, axis=-1, keepdims=True) / D + NORM_EPS
    )
    normed_one = (inputs_f * attention_scale * attention_gain_all).astype(bf16)
    projected = dot(normed_one, qkv_all)

    def prep_local(proj_rows, gain_query, gain_key):
        return prepare(proj_rows, pos_query, gain_query, gain_key)

    (queries, key_part, value_part), prep_back = jax.vjp(
        prep_local, projected, query_gain, key_gain
    )
    queries_b = queries.astype(bf16).transpose(1, 0, 2).reshape(HEADS * per_device, HD)
    kv_local = jnp.concatenate([key_part, value_part], axis=-1).astype(bf16)
    kv_own = gather_tokens(kv_local)
    kv_all = both(kv_own, 0)
    keys_b, values_b = kv_all[:, :HD], kv_all[:, HD:]
    grad_out_own, kv_own_done = lax.optimization_barrier((grad_out_own, kv_own))
    grad_out_all = gather_tokens(grad_out_own)
    out_all = both(out_weight, 1)
    down_all = both(down_weight, 1)
    gate_all = both(gate_weight, 0)
    up_all = both(up_weight, 0)

    def heads_of(rows):
        return rows.reshape(HEADS, per_device, rows.shape[-1])

    scores = heads_of(dot(queries_b, keys_b.T) * scale)
    scores = jnp.where(allowed[None], scores, MASKED_SCORE)
    row_max = jnp.max(scores, axis=-1, keepdims=True)
    row_sum = jnp.sum(jnp.where(allowed[None], jnp.exp(scores - row_max), 0.0), -1, keepdims=True)
    log_total = row_max + jnp.log(row_sum)
    weights = jnp.where(allowed[None], jnp.exp(scores - log_total), 0.0)
    weights_b = weights.astype(bf16).reshape(HEADS * per_device, group_tokens)
    attended = dot(weights_b, values_b)
    attended_b = heads_of(attended).transpose(1, 0, 2).reshape(per_device, HQ).astype(bf16)
    hidden_one = inputs_f + dot(attended_b, out_all)
    feedforward_scale = lax.rsqrt(
        jnp.sum(hidden_one * hidden_one, axis=-1, keepdims=True) / D + NORM_EPS
    )
    normed_two = (hidden_one * feedforward_scale * feedforward_gain_all).astype(bf16)
    normed_all = gather_tokens(normed_two)
    grad_activated = dot(grad_out_all, down_all.T)
    gate_value = dot(normed_all, gate_all)
    upper = dot(normed_all, up_all)
    activated_f, mix_back = jax.vjp(gelu_mix, gate_value, upper)
    activated = activated_f.astype(bf16)
    grad_gate_f, grad_upper_f = mix_back(grad_activated)
    grad_gate = grad_gate_f.astype(bf16)
    grad_upper = grad_upper_f.astype(bf16)
    normed_part = (dot(grad_gate, gate_all.T) + dot(grad_upper, up_all.T)).astype(bf16)
    normed_part, activated, grad_gate, grad_upper = lax.optimization_barrier(
        (normed_part, activated, grad_gate, grad_upper)
    )
    grad_normed_two = scatter_tokens(normed_part)

    def rows_total(rows, columns):
        return dot(rows[:, :width].T, columns) + partner(
            dot(rows[:, width:].T, columns).astype(bf16)
        ).astype(f32)

    grad_gate_weight = sum_dp(rows_total(normed_all, grad_gate))
    grad_up_weight = sum_dp(rows_total(normed_all, grad_upper))
    grad_down_weight = sum_dp(
        dot(activated.T, grad_out_all[:, :width])
        + partner(dot(activated.T, grad_out_all[:, width:]).astype(bf16)).astype(f32)
    )
    down_part = dot(activated, down_all).astype(bf16)

    grad_hidden, ff_gain_part = norm_backward(
        grad_out_own.astype(f32),
        grad_normed_two,
        hidden_one,
        feedforward_scale,
        feedforward_gain_all,
    )
    grad_hidden_b = grad_hidden.astype(bf16)
    grad_attended = (
        dot(grad_hidden_b, out_all.T)
        .reshape(per_device, HEADS, HD)
        .transpose(1, 0, 2)
        .reshape(HEADS * per_device, HD)
    )
    grad_attended_b = grad_attended.astype(bf16)
    correction = heads_of(jnp.sum(grad_attended * attended, axis=-1, keepdims=True))
    grad_weights = heads_of(dot(grad_attended_b, values_b.T))
    grad_scores = (
        (weights * (grad_weights - correction))
        .astype(bf16)
        .reshape(HEADS * per_device, group_tokens)
    )
    grad_queries = heads_of(dot(grad_scores, keys_b) * scale).transpose(1, 0, 2)
    kv_terms = jnp.concatenate(
        [dot(grad_scores.T, queries_b) * scale, dot(weights_b.T, grad_attended_b)], axis=-1
    )
    own_keys = group_tokens // groups_x
    kv_sum = kv_terms[:own_keys] + partner(kv_terms[own_keys:].astype(bf16)).astype(f32)
    kv_grads = scatter_tokens(kv_sum)
    down_part, kv_grads = lax.optimization_barrier((down_part, kv_grads))
    output = to_widths((hidden_one + scatter_tokens(down_part)).astype(bf16))

    out_total = dot(attended_b.T, grad_hidden_b[:, :width]) + partner(
        dot(attended_b.T, grad_hidden_b[:, width:])
    )
    grad_out_weight = lax.psum_scatter(
        rows_scatter_dp(out_total), "gy", scatter_dimension=0, tiled=True
    )
    grad_projected, q_gain_part, k_gain_part = prep_back(
        (grad_queries, kv_grads[:, :HD], kv_grads[:, HD:])
    )
    grad_projected_b = grad_projected.astype(bf16)
    qkv_total = dot(grad_projected_b.T, normed_one[:, :width]) + partner(
        dot(grad_projected_b.T, normed_one[:, width:])
    )
    grad_qkv_weight = lax.psum_scatter(
        rows_scatter_dp(qkv_total), "gy", scatter_dimension=0, tiled=True
    ).T
    grad_normed_one = dot(grad_projected_b, qkv_all.T)
    grad_inputs, att_gain_part = norm_backward(
        grad_hidden, grad_normed_one, inputs_f, attention_scale, attention_gain_all
    )
    gain_own = jnp.concatenate(
        [att_gain_part[:width], ff_gain_part[:width], q_gain_part, k_gain_part]
    )
    gain_other = jnp.concatenate(
        [att_gain_part[width:], ff_gain_part[width:], q_gain_part, k_gain_part]
    )
    gain_sums = small_sum(gain_own + partner(gain_other))
    return (
        output,
        to_widths(grad_inputs),
        gain_sums[:width],
        grad_qkv_weight,
        gain_sums[2 * width : 2 * width + HD],
        gain_sums[2 * width + HD :],
        grad_out_weight,
        gain_sums[width : 2 * width],
        grad_gate_weight,
        grad_up_weight,
        grad_down_weight,
    )


def solution(mesh):
    return jax.shard_map(
        body,
        mesh=mesh,
        in_specs=(
            P(("dp", "gy"), "gx"),
            P("dp"),
            P("dp"),
            P("gx"),
            P("gx", None),
            P(),
            P(),
            P(None, "gx"),
            P("gx"),
            P("gx", "gy"),
            P("gx", "gy"),
            P("gy", "gx"),
            P(("dp", "gy"), "gx"),
        ),
        out_specs=(
            P(("dp", "gy"), "gx"),
            P(("dp", "gy"), "gx"),
            P("gx"),
            P("gx", ("dp", "gy")),
            P(),
            P(),
            P(("dp", "gy"), "gx"),
            P("gx"),
            P("gx", "gy"),
            P("gx", "gy"),
            P("gy", "gx"),
        ),
        check_vma=False,
    )
```
